256 devices in a mesh: rows: 256 (over z, y, x, core).
Axes of the slice: x: 4, y: 4, z: 8, core: 2. Of those that a mesh axis runs over, the one named last changes fastest.
Arguments:
- sketch: float32 [524288, 512], P('rows'), may hold values from -100 to 100
- panel: float32 [524288, 512], P('rows'), may hold values from -24 to 24
Outputs:
- basis: float32 [524288, 512], P('rows')
- projected: float32 [512, 512], P('rows')
The draws below stay inside these ranges and needn't reach their ends.
All inputs are finite; a program needn't handle non-finite values.
Results may differ from the reference program's by a relative error of at most 0.00029.
Values sent between devices are 32-bit elements; how exact they have to be, the bound alone decides.
No kernel may reach another device: no remote copies, remote signals or barrier semaphores. Data moves between devices by JAX's collectives and lax.ppermute only.
A program may use at most 64 MiB of HBM per device.

```python
import jax
import jax.numpy as jnp
from jax import lax

K = 512
F = 512
ROWS = 524288


def draw_sketch(key, part):
    keys = jax.random.split(jax.random.fold_in(key, 7), 2)
    position = jnp.arange(ROWS, dtype=jnp.float32) / ROWS
    growth = jnp.exp(jnp.log(3.0) * position)[:, None]
    col_scale = jnp.exp(jax.random.uniform(keys[1], (1, K), jnp.float32, jnp.log(0.5), jnp.log(2.0)))
    base = jnp.clip(jax.random.normal(keys[0], (ROWS, K), jnp.float32), -6.0, 6.0)
    mixed = base + 0.6 * jnp.roll(base, 1, axis=1)
    values = mixed * col_scale * growth
    return jnp.clip(values, -100.0, 100.0).astype(jnp.float32)


def strengthened(result, own_key, source, target, blocks, factor):
    def block_of(dim):
        return (jnp.arange(result.shape[dim]) // (result.shape[dim] // blocks)).reshape((-1,) + (1,) * (result.ndim - 1 - dim))

    first = jax.random.permutation(own_key, blocks)[block_of(target)]
    other_side = (block_of(target) + blocks // 2) % blocks
    return jnp.where((block_of(source) == first) | (block_of(source) == other_side), factor * result, result)


def block_scale(stream_key, extent, cuts, low, largest):
    level = 1.0
    for axis_at, parts in cuts:
        heights = jax.random.uniform(jax.random.fold_in(jax.random.fold_in(stream_key, 6), axis_at), (parts,), jnp.float32, low / len(cuts), largest / len(cuts))
        level = level * jnp.repeat(jnp.exp(heights), extent[axis_at] // parts).reshape((-1,) + (1,) * (len(extent) - 1 - axis_at))
    return level


def bell_draw_with(stream_key, dims, spread, reach, pieces, heavy, kind=jnp.bfloat16):
    entries = spread * jax.random.normal(stream_key, dims, jnp.float32)
    if pieces:
        entries = entries * block_scale(stream_key, dims, pieces, -0.22, 0.18)
    return jnp.clip(strengthened(entries, jax.random.fold_in(stream_key, 3), *heavy), -reach, reach).astype(kind)


def setup_inputs(seed: int = 0) -> dict:
    arg_keys = jax.random.split(jax.random.key(seed), 3)
    sketch = draw_sketch(jax.random.fold_in(arg_keys[2], 71), 0)
    panel = bell_draw_with(arg_keys[1], (ROWS, F), 1.0, 24.0, ((0, 256),), (0, 1, 256, 6.0), jnp.float32)
    return {"sketch": sketch, "panel": panel}


def reference(sketch, panel):
    highest = lax.Precision.HIGHEST
    gram = lax.dot_general(sketch.astype(jnp.float32), sketch.astype(jnp.float32), (((0,), (0,)), ((), ())), precision=highest, preferred_element_type=jnp.float32) / ROWS
    lower = jnp.linalg.cholesky(gram)
    basis = jax.scipy.linalg.solve_triangular(lower, sketch.T, lower=True).T
    projected = lax.dot_general(panel.astype(jnp.float32), basis.astype(jnp.float32), (((0,), (0,)), ((), ())), precision=highest, preferred_element_type=jnp.float32)
    projected = projected / jnp.sqrt(jnp.float32(ROWS))
    return (basis, projected)
```

```python
import jax
import jax.numpy as jnp
from jax import lax
from jax.experimental import pallas as pl
from jax.experimental.pallas import tpu as pltpu
from jax.sharding import Mesh, PartitionSpec as P


K = 512
B = 128
G = 8
HIGHEST = lax.Precision.HIGHEST
HIGH = lax.Precision.HIGH


def dot(a, b, ca, cb, precision):
    return lax.dot_general(
        a, b, (((ca,), (cb,)), ((), ())), precision=precision, preferred_element_type=jnp.float32
    )


def factor_block(t):
    n = B // G
    lane = lax.broadcasted_iota(jnp.int32, (G, B), 1)
    sub = lax.broadcasted_iota(jnp.int32, (G, B), 0)
    out = []
    for s in range(n):
        c0 = s * G
        tj = t[s]
        col = [jnp.broadcast_to(tj[:, c0 + b : c0 + b + 1], (G, B)) for b in range(G)]
        p = [[None] * G for _ in range(G)]
        for a in range(G):
            for b in range(a, G):
                p[a][b] = jnp.broadcast_to(col[b][a : a + 1, :], (G, B))
        inside = (lane >= c0) & (lane < c0 + G)
        base = jnp.where(inside, jnp.where(lane - c0 == sub, 1.0, 0.0), tj)
        r = [jnp.broadcast_to(base[a : a + 1, :], (G, B)) for a in range(G)]
        dinv = [None] * G
        for b in range(G):
            dinv[b] = 1.0 / p[b][b]
            w = [p[b][a] * dinv[b] for a in range(G)[b + 1 :]]
            for a in range(b + 1, G):
                for c in range(a, G):
                    p[a][c] = p[a][c] - w[a - b - 1] * p[b][c]
                r[a] = r[a] - w[a - b - 1] * r[b]
        rs = [r[a] * lax.rsqrt(p[a][a]) for a in range(G)]
        o = rs[G - 1]
        for a in range(G - 2, -1, -1):
            o = jnp.where(sub == a, rs[a], o)
        out.append(jnp.where(lane <= sub + c0, o, 0.0))
        if s + 1 < n:
            y = [None] * G
            for b in range(G - 1, -1, -1):
                v = r[b] * dinv[b]
                for c in range(b + 1, G):
                    v = v - (p[b][c] * dinv[b]) * y[c]
                y[b] = v
            for g in range(s + 1, n):
                tg = t[g]
                acc = jnp.where(inside, 0.0, tg)
                for b in range(G):
                    acc = acc - jnp.broadcast_to(tg[:, c0 + b : c0 + b + 1], (G, B)) * y[b]
                t[g] = acc
    return out


def factor_kernel(core_ref, mine_ref, other_ref, w_ref, fold_ref, s_ref):
    core = core_ref[0]
    fold_ref[core] = mine_ref[...]
    fold_ref[1 - core] = other_ref[...]
    nb = K // B
    w_ref[...] = jnp.zeros_like(w_ref)
    s_ref[...] = jnp.zeros_like(s_ref)
    s_ref[0:B, :] = fold_ref[0, :, 0:K]
    s_ref[3 * B : 4 * B, 3 * B :] = fold_ref[0, :, K:]
    s_ref[B : 2 * B, B:] = fold_ref[1, :, 0 : 3 * B]
    s_ref[2 * B : 3 * B, 2 * B :] = fold_ref[1, :, 3 * B :]
    for k in range(nb):
        k0, k1 = k * B, (k + 1) * B
        t = [s_ref[k0 + g * G : k0 + (g + 1) * G, k0:k1] for g in range(B // G)]
        for g, rows in enumerate(factor_block(t)):
            w_ref[k0 + g * G : k0 + (g + 1) * G, k0:k1] = rows
        linv = w_ref[k0:k1, k0:k1]
        if k:
            left = dot(linv, s_ref[k0:k1, :k0], 1, 0, HIGHEST)
            w_ref[k0:k1, :k0] = left
        if k + 1 < nb:
            right = dot(linv, s_ref[k0:k1, k1:], 1, 0, HIGHEST)
            for i in range(k + 1, nb):
                lt = right[:, (i - k - 1) * B : (i - k) * B]
                i0, i1 = i * B, (i + 1) * B
                s_ref[i0:i1, i0:] = s_ref[i0:i1, i0:] - dot(lt, right[:, (i - k - 1) * B :], 0, 0, HIGHEST)
                if k:
                    s_ref[i0:i1, :k0] = s_ref[i0:i1, :k0] - dot(lt, left, 0, 0, HIGHEST)
                s_ref[i0:i1, k0:k1] = s_ref[i0:i1, k0:k1] - dot(lt, linv, 0, 0, HIGHEST)


def lower_inverse(core, mine, other):
    vmem = pl.BlockSpec(memory_space=pltpu.VMEM)
    return pl.pallas_call(
        factor_kernel,
        out_shape=jax.ShapeDtypeStruct((K, K), jnp.float32),
        in_specs=[pl.BlockSpec(memory_space=pltpu.SMEM), vmem, vmem],
        out_specs=vmem,
        scratch_shapes=[
            pltpu.VMEM((2, B, K + B), jnp.float32),
            pltpu.VMEM((K, K), jnp.float32),
        ],
        cost_estimate=pl.CostEstimate(flops=400_000_000, bytes_accessed=2_000_000, transcendentals=0),
        name="factor",
    )(core, mine, other)


CHIPS = ("z", "y", "x")


def on_device(sketch, panel):
    core = lax.axis_index("c")
    rows_all = sketch.shape[0] * lax.axis_size(CHIPS + ("c",))
    chips = lax.axis_size(CHIPS)
    swap = [(0, 1), (1, 0)]

    gram = dot(sketch, sketch, 0, 0, HIGH)
    fold = jnp.stack(
        [
            jnp.concatenate([gram[0:B, :], gram[3 * B :, 3 * B :]], axis=1),
            jnp.concatenate([gram[B : 2 * B, B:], gram[2 * B : 3 * B, 2 * B :]], axis=1),
        ]
    )
    keep = lax.dynamic_index_in_dim(fold, core, 0, keepdims=False)
    send = lax.dynamic_index_in_dim(fold, 1 - core, 0, keepdims=False)
    half = keep + lax.ppermute(send, "c", swap)
    got = lax.all_to_all(half.reshape(chips, 1, K + B), CHIPS, 0, 0, tiled=True)
    row = jnp.sum(got, axis=0, keepdims=True) * (1.0 / rows_all)
    mine = lax.all_to_all(
        jnp.broadcast_to(row, (chips, 1, K + B)), CHIPS, 0, 0, tiled=True
    ).reshape(B, K + B)
    other = lax.ppermute(mine, "c", swap)
    winv = lower_inverse(core.reshape(1).astype(jnp.int32), mine, other)

    cross = dot(panel, sketch, 0, 0, HIGH)
    frames = cross.shape[0] // (chips * 2)
    cross = cross.reshape(chips, 2, frames, K)
    ckeep = lax.dynamic_index_in_dim(cross, core, 1, keepdims=False)
    csend = lax.dynamic_index_in_dim(cross, 1 - core, 1, keepdims=False)
    chalf = ckeep + lax.ppermute(csend, "c", swap)
    crows = jnp.sum(lax.all_to_all(chalf, CHIPS, 0, 0, tiled=True), axis=0)

    basis = dot(sketch, winv, 1, 1, HIGH)
    scale = 1.0 / jnp.sqrt(jnp.float32(rows_all))
    projected = dot(crows, winv, 1, 1, HIGHEST) * scale
    return basis, projected


def solution(mesh):
    shape = (8, 4, 4, 2)
    torus = Mesh(mesh.devices.reshape(shape), ("z", "y", "x", "c"))
    spec = P(("z", "y", "x", "c"), None)
    return jax.shard_map(
        on_device,
        mesh=torus,
        in_specs=(spec, spec),
        out_specs=(spec, spec),
        check_vma=False,
    )
```

```python
import functools

import jax
import jax.numpy as jnp
from jax import lax
from jax.experimental import pallas as pl
from jax.experimental.pallas import tpu as pltpu
from jax.sharding import Mesh, PartitionSpec as P


K = 512
B = 128
G = 8


def dot(a, b, ca, cb, precision=None):
    return lax.dot_general(
        a, b, (((ca,), (cb,)), ((), ())), precision=precision, preferred_element_type=jnp.float32
    )


def halves(x):
    hi = x.astype(jnp.bfloat16)
    return hi, (x - hi.astype(jnp.float32)).astype(jnp.bfloat16)


def dot3(a, b, ca, cb):
    a3 = jnp.concatenate([a[0], a[0], a[1]], axis=ca)
    b3 = jnp.concatenate([b[0], b[1], b[0]], axis=cb)
    return dot(a3, b3, ca, cb)


def thirds(x):
    hi = x.astype(jnp.bfloat16)
    rest = x - hi.astype(jnp.float32)
    mid = rest.astype(jnp.bfloat16)
    return hi, mid, (rest - mid.astype(jnp.float32)).astype(jnp.bfloat16)


def left6(x):
    h, m, l = thirds(x)
    return jnp.concatenate([l, h, m, m, h, h], axis=1)


def right6(x):
    h, m, l = thirds(x)
    return jnp.concatenate([h, l, m, h, m, h], axis=0)


def dot6(a6, b6):
    return dot(a6, b6, 1, 0)


def gram_kernel(core_ref, x_ref, keep_ref, send_ref, acc_ref):
    i = pl.program_id(0)
    h = K // 2
    left = halves(x_ref[:, :h])
    right = halves(x_ref[:, h:])
    parts = (dot3(left, left, 0, 0), dot3(left, right, 0, 0), dot3(right, right, 0, 0))

    @pl.when(i == 0)
    def _():
        for j in range(3):
            acc_ref[j] = parts[j]

    @pl.when(i > 0)
    def _():
        for j in range(3):
            acc_ref[j] += parts[j]

    @pl.when(i == pl.num_programs(0) - 1)
    def _():
        def fold(ref, half):
            if half == 0:
                ref[:, 0:h] = acc_ref[0, 0:B, :]
                ref[:, h:K] = acc_ref[1, 0:B, :]
                ref[:, K:] = acc_ref[2, B:, B:]
            else:
                ref[:, 0:B] = acc_ref[0, B:, B:]
                ref[:, B : 3 * B] = acc_ref[1, B:, :]
                ref[:, 3 * B :] = acc_ref[2, 0:B, :]

        for core in range(2):
            @pl.when(core_ref[0] == core)
            def _():
                fold(keep_ref, core)
                fold(send_ref, 1 - core)


def folded_gram(core, sketch, tile=1024):
    rows = sketch.shape[0]
    out = jax.ShapeDtypeStruct((B, K + B), jnp.float32)
    whole = pl.BlockSpec((B, K + B), lambda i: (0, 0))
    return pl.pallas_call(
        gram_kernel,
        out_shape=(out, out),
        grid=(rows // tile,),
        in_specs=[
            pl.BlockSpec(memory_space=pltpu.SMEM),
            pl.BlockSpec((tile, K), lambda i: (i, 0)),
        ],
        out_specs=(whole, whole),
        scratch_shapes=[pltpu.VMEM((3, K // 2, K // 2), jnp.float32)],
        cost_estimate=pl.CostEstimate(
            flops=6 * rows * K * K, bytes_accessed=4 * rows * K, transcendentals=0
        ),
        compiler_params=pltpu.CompilerParams(vmem_limit_bytes=24 << 20),
        name="gram",
    )(core, sketch)


def cross_kernel(p_ref, x_ref, o_ref):
    x = halves(x_ref[...])
    p = halves(p_ref[...])
    part = dot3(p, x, 0, 0)

    @pl.when(pl.program_id(0) == 0)
    def _():
        o_ref[...] = part

    @pl.when(pl.program_id(0) > 0)
    def _():
        o_ref[...] += part


def cross_product(panel, sketch, tile=1024):
    rows, frames = panel.shape
    return pl.pallas_call(
        cross_kernel,
        out_shape=jax.ShapeDtypeStruct((frames, K), jnp.float32),
        grid=(rows // tile,),
        in_specs=[
            pl.BlockSpec((tile, frames), lambda i: (i, 0)),
            pl.BlockSpec((tile, K), lambda i: (i, 0)),
        ],
        out_specs=pl.BlockSpec((frames, K), lambda i: (0, 0)),
        cost_estimate=pl.CostEstimate(
            flops=6 * rows * K * frames, bytes_accessed=8 * rows * K, transcendentals=0
        ),
        compiler_params=pltpu.CompilerParams(vmem_limit_bytes=28 << 20),
        name="cross",
    )(panel, sketch)


def factor_block(t, bc_ref):
    n = B // G
    lane = lax.broadcasted_iota(jnp.int32, (G, B), 1)
    sub = lax.broadcasted_iota(jnp.int32, (G, B), 0)
    out = []
    for s in range(n):
        c0 = s * G
        tj = t[s]
        ahead = s + 1 < n

        def lanes_of(v, b):
            return jnp.broadcast_to(v[:, c0 + b : c0 + b + 1], (G, B))

        inside = (lane >= c0) & (lane < c0 + G)
        m = []
        for b in range(G):
            bc_ref[s, b] = lanes_of(tj, b)
            if ahead:
                m.append(lanes_of(t[s + 1], b))
        bc_ref[s, G] = jnp.where(inside, jnp.where(lane - c0 == sub, 1.0, 0.0), tj)
        p = [[None] * G for _ in range(G)]
        for b in range(G):
            for a in range(b + 1):
                p[a][b] = bc_ref[s, b, pl.ds(a, G, stride=0), :]
        r = [bc_ref[s, G, pl.ds(a, G, stride=0), :] for a in range(G)]
        if ahead:
            acc = jnp.where(inside, 0.0, t[s + 1])
        dinv = [None] * G
        for b in range(G):
            d = 1.0 / p[b][b]
            dinv[b] = d
            if b + 1 < G:
                p[b + 1][b + 1] = p[b + 1][b + 1] - (p[b][b + 1] * p[b][b + 1]) * d
            for a in range(b + 1, G):
                w = p[b][a] * d
                for c in range(a, G):
                    if (a, c) != (b + 1, b + 1):
                        p[a][c] = p[a][c] - w * p[b][c]
                r[a] = r[a] - w * r[b]
            if ahead:
                u = m[b] * d
                for c in range(b + 1, G):
                    m[c] = m[c] - u * p[b][c]
                acc = acc - u * r[b]
        if ahead:
            y = [None] * G
            for b in range(G - 1, -1, -1):
                v = r[b] * dinv[b]
                for c in range(b + 1, G):
                    v = v - (p[b][c] * dinv[b]) * y[c]
                y[b] = v
            rest = [jnp.where(inside, 0.0, t[g]) for g in range(s + 2, n)]
            for b in range(G - 1, -1, -1):
                for i, g in enumerate(range(s + 2, n)):
                    rest[i] = rest[i] - lanes_of(t[g], b) * y[b]
            t[s + 1] = acc
            t[s + 2 :] = rest
        rs = [r[a] * lax.rsqrt(p[a][a]) for a in range(G)]
        o = rs[G - 1]
        for a in range(G - 2, -1, -1):
            o = jnp.where(sub == a, rs[a], o)
        out.append(jnp.where(lane <= sub + c0, o, 0.0))
    return out


def factor_kernel(core_ref, mine_ref, other_ref, w_ref, fold_ref, s_ref, bc_ref):
    core = core_ref[0]
    fold_ref[core] = mine_ref[...]
    fold_ref[1 - core] = other_ref[...]
    nb = K // B
    s_ref[0:B, :] = fold_ref[0, :, 0:K]
    s_ref[3 * B : 4 * B, 3 * B :] = fold_ref[0, :, K:]
    s_ref[B : 2 * B, B:] = fold_ref[1, :, 0 : 3 * B]
    s_ref[2 * B : 3 * B, 2 * B :] = fold_ref[1, :, 3 * B :]
    for i in range(1, nb):
        s_ref[i * B : (i + 1) * B, : i * B] = jnp.zeros((B, i * B), jnp.float32)
    for k in range(nb):
        k0, k1, k2 = k * B, (k + 1) * B, (k + 2) * B
        last = k + 1 == nb
        t = [s_ref[k0 + g * G : k0 + (g + 1) * G, k0:k1] for g in range(B // G)]
        for g, rows in enumerate(factor_block(t, bc_ref)):
            w_ref[k0 + g * G : k0 + (g + 1) * G, k0:k1] = rows
        linv = w_ref[k0:k1, k0:k1]
        linv6 = left6(linv)
        if not last:
            w_ref[k0:k1, k1:] = jnp.zeros((B, K - k1), jnp.float32)
            near = dot6(linv6, right6(s_ref[k0:k1, k1:k2]))
            near6 = left6(near.T)
            s_ref[k1:k2, k1:k2] = s_ref[k1:k2, k1:k2] - dot6(near6, right6(near))
        if k:
            left = dot6(linv6, right6(s_ref[k0:k1, :k0]))
            w_ref[k0:k1, :k0] = left
        if not last:
            done = [left, linv] if k else [linv]
            done6 = right6(jnp.concatenate(done, axis=1))
            if k + 2 < nb:
                far = dot6(linv6, right6(s_ref[k0:k1, k2:]))
                far6 = right6(far)
            for i in range(k + 1, nb):
                i0, i1 = i * B, (i + 1) * B
                if i == k + 1:
                    lt6 = near6
                else:
                    f0 = (i - k - 2) * B
                    lt6 = left6(far[:, f0 : f0 + B].T)
                s_ref[i0:i1, :k1] = s_ref[i0:i1, :k1] - dot6(lt6, done6)
                if k + 2 < nb:
                    j0 = max(i, k + 2) * B
                    s_ref[i0:i1, j0:] = s_ref[i0:i1, j0:] - dot6(lt6, far6[:, j0 - k2 :])


def lower_inverse(core, mine, other):
    vmem = pl.BlockSpec(memory_space=pltpu.VMEM)
    return pl.pallas_call(
        factor_kernel,
        out_shape=jax.ShapeDtypeStruct((K, K), jnp.float32),
        in_specs=[pl.BlockSpec(memory_space=pltpu.SMEM), vmem, vmem],
        out_specs=vmem,
        scratch_shapes=[
            pltpu.VMEM((2, B, K + B), jnp.float32),
            pltpu.VMEM((K, K), jnp.float32),
            pltpu.VMEM((B // G, G + 1, G, B), jnp.float32),
        ],
        cost_estimate=pl.CostEstimate(flops=8_000_000_000, bytes_accessed=2_000_000, transcendentals=0),
        compiler_params=pltpu.CompilerParams(vmem_limit_bytes=12 << 20),
        name="factor",
    )(core, mine, other)


def basis_kernel(scale, x_ref, w_ref, c_ref, o_ref, q_ref, hi_ref, lo_ref):
    h = K // 2

    def times(rows):
        rl, rr = halves(rows[:, :h]), halves(rows[:, h:])
        wl = (hi_ref[:h, :h], lo_ref[:h, :h])
        wr = (hi_ref[h:, :h], lo_ref[h:, :h]), (hi_ref[h:, h:], lo_ref[h:, h:])
        return dot3(rl, wl, 1, 1), dot3(rl, wr[0], 1, 1) + dot3(rr, wr[1], 1, 1)

    @pl.when(pl.program_id(0) == 0)
    def _():
        hi_ref[...], lo_ref[...] = halves(w_ref[...])
        left, right = times(c_ref[...])
        q_ref[:, :h] = left * scale
        q_ref[:, h:] = right * scale

    o_ref[:, :h], o_ref[:, h:] = times(x_ref[...])


def apply_inverse(sketch, winv, crows, scale, tile=1024):
    rows = sketch.shape[0]
    n = crows.shape[0]
    fixed = pl.BlockSpec((K, K), lambda i: (0, 0))
    small = pl.BlockSpec((n, K), lambda i: (0, 0))
    return pl.pallas_call(
        functools.partial(basis_kernel, scale),
        out_shape=(
            jax.ShapeDtypeStruct((rows, K), jnp.float32),
            jax.ShapeDtypeStruct((n, K), jnp.float32),
        ),
        grid=(rows // tile,),
        in_specs=[pl.BlockSpec((tile, K), lambda i: (i, 0)), fixed, small],
        out_specs=(pl.BlockSpec((tile, K), lambda i: (i, 0)), small),
        scratch_shapes=[pltpu.VMEM((K, K), jnp.bfloat16)] * 2,
        cost_estimate=pl.CostEstimate(
            flops=6 * rows * K * K, bytes_accessed=8 * rows * K, transcendentals=0
        ),
        compiler_params=pltpu.CompilerParams(vmem_limit_bytes=24 << 20),
        name="basis",
    )(sketch, winv, crows)


PLANE = ("y", "x")
SWAP = [(0, 1), (1, 0)]


def shift(x, by, n):
    return lax.ppermute(x, "z", [(i, (i + by) % n) for i in range(n)])


def sum_over_ring(x):
    n = lax.axis_size("z")
    before = shift(x, 1, n)
    after = shift(x, -1, n)
    two = x + before
    three = two + after
    return three + shift(three, 3, n) + shift(two, -3, n)


def on_device(sketch, panel):
    core = lax.axis_index("c").astype(jnp.int32)
    plane = lax.axis_size(PLANE)
    ring = lax.axis_size("z")
    rows_all = sketch.shape[0] * plane * ring * 2

    keep, send = folded_gram(core.reshape(1), sketch)
    half = keep + lax.ppermute(send, "c", SWAP)
    got = lax.all_to_all(half.reshape(plane, B // plane, K + B), PLANE, 0, 0, tiled=True)
    part = sum_over_ring(jnp.sum(got, axis=0)) * (1.0 / rows_all)
    mine = lax.all_to_all(
        jnp.broadcast_to(part, (plane,) + part.shape), PLANE, 0, 0, tiled=True
    ).reshape(B, K + B)
    other = lax.ppermute(mine, "c", SWAP)
    winv = lower_inverse(core.reshape(1), mine, other)

    cross = cross_product(panel, sketch)
    frames = cross.shape[0] // (ring * plane * 2)
    cross = cross.reshape(ring, plane, 2, frames, K)
    ckeep = lax.dynamic_index_in_dim(cross, core, 2, keepdims=False)
    csend = lax.dynamic_index_in_dim(cross, 1 - core, 2, keepdims=False)
    chalf = ckeep + lax.ppermute(csend, "c", SWAP)
    chalf = chalf.transpose(1, 0, 2, 3).reshape(plane, ring * frames, K)
    got = lax.all_to_all(chalf, PLANE, 0, 0, tiled=True)
    crows = jnp.sum(got, axis=0).reshape(ring, frames, K)
    got = lax.all_to_all(crows, "z", 0, 0, tiled=True)
    crows = jnp.sum(got, axis=0)

    return apply_inverse(sketch, winv, crows, rows_all ** -0.5)


def solution(mesh):
    torus = Mesh(mesh.devices.reshape(8, 4, 4, 2), ("z", "y", "x", "c"))
    spec = P(("z", "y", "x", "c"), None)

    return jax.shard_map(
        on_device,
        mesh=torus,
        in_specs=(spec, spec),
        out_specs=(spec, spec),
        check_vma=False,
    )
```

```python
import functools

import jax
import jax.numpy as jnp
from jax import lax
from jax.experimental import pallas as pl
from jax.experimental.pallas import tpu as pltpu
from jax.sharding import Mesh, PartitionSpec as P


K = 512
B = 128
G = 8


def dot(a, b, ca, cb, precision=None):
    return lax.dot_general(
        a, b, (((ca,), (cb,)), ((), ())), precision=precision, preferred_element_type=jnp.float32
    )


def halves(x):
    hi = x.astype(jnp.bfloat16)
    return hi, (x - hi.astype(jnp.float32)).astype(jnp.bfloat16)


def dot3(a, b, ca, cb):
    a3 = jnp.concatenate([a[0], a[0], a[1]], axis=ca)
    b3 = jnp.concatenate([b[0], b[1], b[0]], axis=cb)
    return dot(a3, b3, ca, cb)


def thirds(x):
    hi = x.astype(jnp.bfloat16)
    rest = x - hi.astype(jnp.float32)
    mid = rest.astype(jnp.bfloat16)
    return hi, mid, (rest - mid.astype(jnp.float32)).astype(jnp.bfloat16)


def left6(x):
    h, m, l = thirds(x)
    return jnp.concatenate([l, h, m, m, h, h], axis=1)


def right6(x):
    h, m, l = thirds(x)
    return jnp.concatenate([h, l, m, h, m, h], axis=0)


def dot6(a6, b6):
    return dot(a6, b6, 1, 0)


VMEM = pl.BlockSpec(memory_space=pltpu.VMEM)
SMEM = pl.BlockSpec(memory_space=pltpu.SMEM)
HBM = pl.BlockSpec(memory_space=pltpu.HBM)


def start_loads(pairs, sems, sizes):
    loads, start = [], 0
    for i, size in enumerate(sizes):
        at = pl.ds(start, size)
        loads.append(
            [pltpu.make_async_copy(src.at[at], dst.at[at], sems.at[j, i]) for j, (src, dst) in enumerate(pairs)]
        )
        for load in loads[-1]:
            load.start()
        start += size
    return loads


GRAM_STEPS = (256, 256, 512, 512, 512)
CROSS_STEPS = (256, 256, 512, 1024)
BASIS_STEPS = (256, 256, 512, 512, 256, 256)


def gram_kernel(core_ref, x_hbm, keep_ref, send_ref, x_ref, acc_ref, sems):
    loads = start_loads(((x_hbm, x_ref),), sems, GRAM_STEPS)
    h = K // 2
    start = 0
    for i, size in enumerate(GRAM_STEPS):
        loads[i][0].wait()
        rows = slice(start, start + size)
        start += size
        left = halves(x_ref[rows, :h])
        right = halves(x_ref[rows, h:])
        parts = (dot3(left, left, 0, 0), dot3(left, right, 0, 0), dot3(right, right, 0, 0))
        for j in range(3):
            acc_ref[j] = parts[j] if i == 0 else acc_ref[j] + parts[j]

    def fold(ref, half):
        if half == 0:
            ref[:, 0:h] = acc_ref[0, 0:B, :]
            ref[:, h:K] = acc_ref[1, 0:B, :]
            ref[:, K:] = acc_ref[2, B:, B:]
        else:
            ref[:, 0:B] = acc_ref[0, B:, B:]
            ref[:, B : 3 * B] = acc_ref[1, B:, :]
            ref[:, 3 * B :] = acc_ref[2, 0:B, :]

    for core in range(2):
        @pl.when(core_ref[0] == core)
        def _():
            fold(keep_ref, core)
            fold(send_ref, 1 - core)


def folded_gram(core, sketch):
    rows = sketch.shape[0]
    half = jax.ShapeDtypeStruct((B, K + B), jnp.float32)
    return pl.pallas_call(
        gram_kernel,
        out_shape=(half, half),
        in_specs=[SMEM, HBM],
        out_specs=(VMEM, VMEM),
        scratch_shapes=[
            pltpu.VMEM(sketch.shape, jnp.float32),
            pltpu.VMEM((3, K // 2, K // 2), jnp.float32),
            pltpu.SemaphoreType.DMA((1, len(GRAM_STEPS))),
        ],
        cost_estimate=pl.CostEstimate(
            flops=6 * rows * K * K, bytes_accessed=4 * rows * K, transcendentals=0
        ),
        compiler_params=pltpu.CompilerParams(vmem_limit_bytes=52 << 20),
        name="gram",
    )(core, sketch)


def cross_kernel(core_ref, p_hbm, x_hbm, keep_ref, send_ref, p_ref, x_ref, acc_ref, sems):
    loads = start_loads(((p_hbm, p_ref), (x_hbm, x_ref)), sems, CROSS_STEPS)
    start = 0
    for i, size in enumerate(CROSS_STEPS):
        for load in loads[i]:
            load.wait()
        rows = slice(start, start + size)
        start += size
        part = dot3(halves(p_ref[rows, :]), halves(x_ref[rows, :]), 0, 0)
        acc_ref[...] = part if i == 0 else acc_ref[...] + part
    plane, ring = keep_ref.shape[0], keep_ref.shape[1] // 2

    def pack(ref, core):
        for z in range(ring):
            for d in range(plane):
                f = (z * plane + d) * 4 + core * 2
                ref[d, 2 * z : 2 * z + 2, :] = acc_ref[f : f + 2, :]

    for core in range(2):
        @pl.when(core_ref[0] == core)
        def _():
            pack(keep_ref, core)
            pack(send_ref, 1 - core)


def cross_product(core, panel, sketch, plane, ring):
    rows, frames = panel.shape
    half = jax.ShapeDtypeStruct((plane, 2 * ring, K), jnp.float32)
    return pl.pallas_call(
        cross_kernel,
        out_shape=(half, half),
        in_specs=[SMEM, HBM, HBM],
        out_specs=(VMEM, VMEM),
        scratch_shapes=[
            pltpu.VMEM(panel.shape, jnp.float32),
            pltpu.VMEM(sketch.shape, jnp.float32),
            pltpu.VMEM((frames, K), jnp.float32),
            pltpu.SemaphoreType.DMA((2, len(CROSS_STEPS))),
        ],
        cost_estimate=pl.CostEstimate(
            flops=6 * rows * K * frames, bytes_accessed=8 * rows * K, transcendentals=0
        ),
        compiler_params=pltpu.CompilerParams(vmem_limit_bytes=52 << 20),
        name="cross",
    )(core, panel, sketch)


def factor_block(t, bc_ref):
    n = B // G
    lane = lax.broadcasted_iota(jnp.int32, (G, B), 1)
    sub = lax.broadcasted_iota(jnp.int32, (G, B), 0)
    out = []
    for s in range(n):
        c0 = s * G
        tj = t[s]
        ahead = s + 1 < n

        def lanes_of(v, b):
            return jnp.broadcast_to(v[:, c0 + b : c0 + b + 1], (G, B))

        inside = (lane >= c0) & (lane < c0 + G)
        m = []
        for b in range(G):
            bc_ref[s, b] = lanes_of(tj, b)
            if ahead:
                m.append(lanes_of(t[s + 1], b))
        bc_ref[s, G] = jnp.where(inside, jnp.where(lane - c0 == sub, 1.0, 0.0), tj)
        p = [[None] * G for _ in range(G)]
        for b in range(G):
            for a in range(b + 1):
                p[a][b] = bc_ref[s, b, pl.ds(a, G, stride=0), :]
        r = [bc_ref[s, G, pl.ds(a, G, stride=0), :] for a in range(G)]
        if ahead:
            acc = jnp.where(inside, 0.0, t[s + 1])
        dinv = [None] * G
        for b in range(G):
            d = 1.0 / p[b][b]
            dinv[b] = d
            if b + 1 < G:
                p[b + 1][b + 1] = p[b + 1][b + 1] - (p[b][b + 1] * p[b][b + 1]) * d
            for a in range(b + 1, G):
                w = p[b][a] * d
                for c in range(a, G):
                    if (a, c) != (b + 1, b + 1):
                        p[a][c] = p[a][c] - w * p[b][c]
                r[a] = r[a] - w * r[b]
            if ahead:
                u = m[b] * d
                for c in range(b + 1, G):
                    m[c] = m[c] - u * p[b][c]
                acc = acc - u * r[b]
        if ahead:
            y = [None] * G
            for b in range(G - 1, -1, -1):
                v = r[b] * dinv[b]
                for c in range(b + 1, G):
                    v = v - (p[b][c] * dinv[b]) * y[c]
                y[b] = v
            rest = [jnp.where(inside, 0.0, t[g]) for g in range(s + 2, n)]
            for b in range(G - 1, -1, -1):
                for i, g in enumerate(range(s + 2, n)):
                    rest[i] = rest[i] - lanes_of(t[g], b) * y[b]
            t[s + 1] = acc
            t[s + 2 :] = rest
        rs = [r[a] * lax.rsqrt(p[a][a]) for a in range(G)]
        o = rs[G - 1]
        for a in range(G - 2, -1, -1):
            o = jnp.where(sub == a, rs[a], o)
        out.append(jnp.where(lane <= sub + c0, o, 0.0))
    return out


def factor_kernel(core_ref, mine_ref, other_ref, w_ref, fold_ref, s_ref, bc_ref):
    core = core_ref[0]
    fold_ref[core] = mine_ref[...]
    fold_ref[1 - core] = other_ref[...]
    nb = K // B
    s_ref[0:B, :] = fold_ref[0, :, 0:K]
    s_ref[3 * B : 4 * B, 3 * B :] = fold_ref[0, :, K:]
    s_ref[B : 2 * B, B:] = fold_ref[1, :, 0 : 3 * B]
    s_ref[2 * B : 3 * B, 2 * B :] = fold_ref[1, :, 3 * B :]
    for i in range(1, nb):
        s_ref[i * B : (i + 1) * B, : i * B] = jnp.zeros((B, i * B), jnp.float32)
    for k in range(nb):
        k0, k1, k2 = k * B, (k + 1) * B, (k + 2) * B
        last = k + 1 == nb
        t = [s_ref[k0 + g * G : k0 + (g + 1) * G, k0:k1] for g in range(B // G)]
        for g, rows in enumerate(factor_block(t, bc_ref)):
            w_ref[k0 + g * G : k0 + (g + 1) * G, k0:k1] = rows
        linv = w_ref[k0:k1, k0:k1]
        linv6 = left6(linv)
        if not last:
            w_ref[k0:k1, k1:] = jnp.zeros((B, K - k1), jnp.float32)
            near = dot6(linv6, right6(s_ref[k0:k1, k1:k2]))
            near6 = left6(near.T)
            s_ref[k1:k2, k1:k2] = s_ref[k1:k2, k1:k2] - dot6(near6, right6(near))
        if k:
            left = dot6(linv6, right6(s_ref[k0:k1, :k0]))
            w_ref[k0:k1, :k0] = left
        if not last:
            done = [left, linv] if k else [linv]
            done6 = right6(jnp.concatenate(done, axis=1))
            if k + 2 < nb:
                far = dot6(linv6, right6(s_ref[k0:k1, k2:]))
                far6 = right6(far)
            for i in range(k + 1, nb):
                i0, i1 = i * B, (i + 1) * B
                if i == k + 1:
                    lt6 = near6
                else:
                    f0 = (i - k - 2) * B
                    lt6 = left6(far[:, f0 : f0 + B].T)
                s_ref[i0:i1, :k1] = s_ref[i0:i1, :k1] - dot6(lt6, done6)
                if k + 2 < nb:
                    j0 = max(i, k + 2) * B
                    s_ref[i0:i1, j0:] = s_ref[i0:i1, j0:] - dot6(lt6, far6[:, j0 - k2 :])


def lower_inverse(core, mine, other):
    return pl.pallas_call(
        factor_kernel,
        out_shape=jax.ShapeDtypeStruct((K, K), jnp.float32),
        in_specs=[SMEM, VMEM, VMEM],
        out_specs=VMEM,
        scratch_shapes=[
            pltpu.VMEM((2, B, K + B), jnp.float32),
            pltpu.VMEM((K, K), jnp.float32),
            pltpu.VMEM((B // G, G + 1, G, B), jnp.float32),
        ],
        cost_estimate=pl.CostEstimate(flops=8_000_000_000, bytes_accessed=2_000_000, transcendentals=0),
        compiler_params=pltpu.CompilerParams(vmem_limit_bytes=8 << 20),
        name="factor",
    )(core, mine, other)


def basis_kernel(scale, x_hbm, w_ref, c_ref, o_hbm, q_ref, x_ref, o_ref, in_sems, out_sems):
    loads = start_loads(((x_hbm, x_ref),), in_sems, BASIS_STEPS)
    h = K // 2
    hi, lo = halves(w_ref[...])
    wl = (hi[:h, :h], lo[:h, :h])
    wr = (hi[h:, :], lo[h:, :])

    def times(rows):
        hi, lo = halves(rows)
        return dot3((hi[:, :h], lo[:, :h]), wl, 1, 1), dot3((hi, lo), wr, 1, 1)

    left, right = times(c_ref[...])
    q_ref[:, :h] = left * scale
    q_ref[:, h:] = right * scale
    stores = []
    start = 0
    for i, size in enumerate(BASIS_STEPS):
        loads[i][0].wait()
        rows = slice(start, start + size)
        o_ref[rows, :h], o_ref[rows, h:] = times(x_ref[rows, :])
        at = pl.ds(start, size)
        stores.append(pltpu.make_async_copy(o_ref.at[at], o_hbm.at[at], out_sems.at[i]))
        stores[-1].start()
        start += size
    for store in stores:
        store.wait()


def apply_inverse(sketch, winv, crows, scale):
    rows = sketch.shape[0]
    n = crows.shape[0]
    return pl.pallas_call(
        functools.partial(basis_kernel, scale),
        out_shape=(
            jax.ShapeDtypeStruct((rows, K), jnp.float32),
            jax.ShapeDtypeStruct((n, K), jnp.float32),
        ),
        in_specs=[HBM, VMEM, VMEM],
        out_specs=(HBM, VMEM),
        scratch_shapes=[
            pltpu.VMEM((rows, K), jnp.float32),
            pltpu.VMEM((rows, K), jnp.float32),
            pltpu.SemaphoreType.DMA((1, len(BASIS_STEPS))),
            pltpu.SemaphoreType.DMA((len(BASIS_STEPS),)),
        ],
        cost_estimate=pl.CostEstimate(
            flops=6 * rows * K * K, bytes_accessed=8 * rows * K, transcendentals=0
        ),
        compiler_params=pltpu.CompilerParams(vmem_limit_bytes=50 << 20),
        name="basis",
    )(sketch, winv, crows)


PLANE = ("y", "x")
SWAP = [(0, 1), (1, 0)]


def shift(x, by, n):
    return lax.ppermute(x, "z", [(i, (i + by) % n) for i in range(n)])


def sum_over_ring(x):
    n = lax.axis_size("z")
    before = shift(x, 1, n)
    after = shift(x, -1, n)
    two = x + before
    three = two + after
    return three + shift(three, 3, n) + shift(two, -3, n)


def on_device(sketch, panel):
    core = lax.axis_index("c").astype(jnp.int32)
    plane = lax.axis_size(PLANE)
    ring = lax.axis_size("z")
    rows_all = sketch.shape[0] * plane * ring * 2

    keep, send = folded_gram(core.reshape(1), sketch)
    half = keep + lax.ppermute(send, "c", SWAP)
    got = lax.all_to_all(half.reshape(plane, B // plane, K + B), PLANE, 0, 0, tiled=True)
    part = sum_over_ring(jnp.sum(got, axis=0)) * (1.0 / rows_all)
    mine = lax.all_to_all(
        jnp.broadcast_to(part, (plane,) + part.shape), PLANE, 0, 0, tiled=True
    ).reshape(B, K + B)
    other = lax.ppermute(mine, "c", SWAP)
    winv = lower_inverse(core.reshape(1), mine, other)

    frames = panel.shape[1] // (ring * plane * 2)
    ckeep, csend = cross_product(core.reshape(1), panel, sketch, plane, ring)
    chalf = ckeep + lax.ppermute(csend, "c", SWAP)
    got = lax.all_to_all(chalf, PLANE, 0, 0, tiled=True)
    crows = jnp.sum(got, axis=0).reshape(ring, frames, K)
    got = lax.all_to_all(crows, "z", 0, 0, tiled=True)
    crows = jnp.sum(got, axis=0)

    return apply_inverse(sketch, winv, crows, rows_all ** -0.5)


def solution(mesh):
    torus = Mesh(mesh.devices.reshape(8, 4, 4, 2), ("z", "y", "x", "c"))
    spec = P(("z", "y", "x", "c"), None)

    return jax.shard_map(
        on_device,
        mesh=torus,
        in_specs=(spec, spec),
        out_specs=(spec, spec),
        check_vma=False,
    )
```
